128 devices in a mesh: chan: 32 (over x, z_hi, y), grp: 4 (over z_lo, core).
Axes of the slice: x: 4, y: 4, z: 4 (z_hi: 2, z_lo: 2; z = z_hi * 2 + z_lo), core: 2. Of those that a mesh axis runs over, the one named last changes fastest.
Arguments:
- voltages: bfloat16 [512, 4096, 128], P(('chan', 'grp')), may hold values from -6 to 6
- delays: int32 [64, 512], replicated, may hold values from 0 to 4095
- shifts: int32 [256, 512], replicated, may hold values from 0 to 511
Outputs:
- dm_power: float32 [256, 512, 256], P('grp', 'chan')
The draws below stay inside these ranges and needn't reach their ends.
All inputs are finite; a program needn't handle non-finite values.
Results may differ from the reference program's by a relative error of at most 0.011.
Values may be sent and summed in bfloat16 or wider, within the bound.
No kernel may reach another device: no remote copies, remote signals or barrier semaphores. Data moves between devices by JAX's collectives and lax.ppermute only.
A program may use at most 128 MiB of HBM per device.

```python
import math
import jax
import jax.numpy as jnp
from jax import lax

DISHES = 64
BEAMS = 512
TIME = 4096
INTEG = 8
DM = 256
PHASES = 4096
KBLK = 16
CHANNELS = 512
TI = 512


def touch_ends(values, own_key, smallest, high):
    dims = values.shape
    index_at = [jax.random.randint(jax.random.fold_in(own_key, axis), (), 0, dims[axis]) for axis in range(len(dims))]
    values = values.at[tuple(index_at)].set(smallest)
    longest = dims.index(max(dims))
    index_at[longest] = (index_at[longest] + 1) % dims[longest]
    return values.at[tuple(index_at)].set(high)


def shard_levels(rng, extent, split, least, top_value):
    def one(dim, shards_of):
        draws = jax.random.uniform(jax.random.fold_in(jax.random.fold_in(rng, 6), dim), (shards_of,), jnp.float32, least / len(split), top_value / len(split))
        return jnp.repeat(jnp.exp(draws), extent[dim] // shards_of).reshape((-1,) + (1,) * (len(extent) - dim - 1))

    level = one(*split[0])
    for cut in split[1:]:
        level = level * one(*cut)
    return level


def scatter_about(stream_key, shape, deviation, most, cuts=(), kind=jnp.bfloat16):
    entries = jax.random.normal(stream_key, shape, jnp.float32) * deviation
    if len(cuts) > 0:
        entries = shard_levels(stream_key, shape, cuts, -0.22, 0.18) * entries
    return jnp.clip(entries, min=-most, max=most).astype(kind)


def setup_inputs(seed: int = 0) -> dict:
    keys = jax.random.split(jax.random.key(seed), 4)
    return {
        "voltages": scatter_about(keys[0], (CHANNELS, TIME, 2 * DISHES), 1.0, 6.0, ((0, 128),)),
        "delays": touch_ends(jax.random.randint(keys[1], (DISHES, BEAMS), 0, PHASES), jax.random.fold_in(keys[1], 1), 0, PHASES - 1).astype(jnp.int32),
        "shifts": touch_ends(jax.random.randint(keys[2], (DM, CHANNELS), 0, TI), jax.random.fold_in(keys[2], 1), 0, TI - 1).astype(jnp.int32),
    }


def beam_matrix(delays, channel, channel_count):
    frequency = (channel + channel_count).astype(jnp.int32)
    residue = jnp.mod(delays * frequency, PHASES)
    phases = residue.astype(jnp.float32) * jnp.float32(2.0 * math.pi / PHASES)
    weight_scale = jnp.float32(1.0 / math.sqrt(DISHES))
    real_part = jnp.cos(phases) * weight_scale
    imag_part = -jnp.sin(phases) * weight_scale
    upper = jnp.concatenate([real_part, imag_part], axis=1)
    lower = jnp.concatenate([-imag_part, real_part], axis=1)
    return jnp.concatenate([upper, lower], axis=0).astype(jnp.bfloat16)

def detect(samples, matrix):
    beams = jnp.dot(samples, matrix, preferred_element_type=jnp.float32)
    half_width = matrix.shape[1] // 2
    intensity = beams[:, :half_width] ** 2 + beams[:, half_width:] ** 2
    steps_count = samples.shape[0] // INTEG
    averaged = lax.optimization_barrier(jnp.sum(intensity.reshape(steps_count, INTEG, half_width), axis=1)) * jnp.float32(1.0 / INTEG)
    return averaged.T.astype(jnp.bfloat16)

def dft_table(length):
    bins_count = length // 2
    sample_index = jnp.arange(length, dtype=jnp.int32)[:, None]
    freq_index = jnp.arange(1, bins_count + 1, dtype=jnp.int32)[None, :]
    residue = jnp.mod(sample_index * freq_index, length)
    phases = residue.astype(jnp.float32) * jnp.float32(2.0 * math.pi / length)
    norm_scale = jnp.float32(1.0 / math.sqrt(length))
    return jnp.concatenate([jnp.cos(phases) * norm_scale, -jnp.sin(phases) * norm_scale], axis=1).astype(jnp.bfloat16)

def spectra(series, table):
    flat = series.reshape(-1, series.shape[-1])
    result = jnp.dot(flat, table, preferred_element_type=jnp.float32).astype(jnp.bfloat16)
    return result.reshape(series.shape[:-1] + (table.shape[1],))

def dedisperse(spectrum, selected, phase_scale):
    channel_count, beam_count, doubled = spectrum.shape
    bins_count = doubled // 2
    trial_count = selected.shape[0]
    stacked = spectrum.reshape(channel_count, beam_count, 2, bins_count).transpose(3, 2, 0, 1)
    stacked = stacked.reshape(bins_count, 2 * channel_count, beam_count)

    def one_block(block_index):
        start = block_index * KBLK
        piece = lax.dynamic_slice_in_dim(stacked, start, KBLK, 0)
        freq_index = (start + jnp.arange(KBLK, dtype=jnp.int32) + 1)[:, None, None]
        residue = jnp.mod(freq_index * selected[None, :, :], doubled)
        phases = residue.astype(jnp.float32) * jnp.float32(2.0 * math.pi / doubled)
        cosine = jnp.cos(phases) * phase_scale
        sine = jnp.sin(phases) * phase_scale
        upper = jnp.concatenate([cosine, -sine], axis=2)
        lower = jnp.concatenate([sine, cosine], axis=2)
        factors = jnp.concatenate([upper, lower], axis=1).astype(jnp.bfloat16)
        return jnp.einsum('kec,kcb->keb', factors.astype(jnp.float32), piece.astype(jnp.float32))
    blocks = lax.map(one_block, jnp.arange(bins_count // KBLK, dtype=jnp.int32))
    return blocks.reshape(bins_count, 2, trial_count, beam_count)

def reference(voltages, delays, shifts):
    table = dft_table(TI)

    def per_channel(item):
        samples, channel = item
        return spectra(detect(samples, beam_matrix(delays, channel, CHANNELS)), table)
    spectrum = lax.map(per_channel, (voltages, jnp.arange(CHANNELS, dtype=jnp.int32)))
    dedispersed = dedisperse(spectrum, shifts, jnp.float32(1.0 / math.sqrt(CHANNELS)))
    result = dedispersed[:, 0] ** 2 + dedispersed[:, 1] ** 2
    return result.transpose(1, 2, 0)
```

```python
import math

import jax
import jax.numpy as jnp
from jax import lax
from jax.experimental import pallas as pl
from jax.experimental.pallas import tpu as pltpu
from jax.sharding import PartitionSpec as P

INTEG = 8
PHASES = 4096
KBLK = 16
CHUNKS = 4
VMEM_LIMIT = 56 * 1024 * 1024


def sin_cos(steps, turn):
    quarter = turn // 4
    steps = steps & (turn - 1)
    quadrant = (steps + quarter // 2) >> (quarter.bit_length() - 1)
    x = (steps - quadrant * quarter).astype(jnp.float32) * jnp.float32(2.0 * math.pi / turn)
    y = x * x
    s = x * (1.0 + y * (-1.0 / 6 + y * (1.0 / 120 + y * (-1.0 / 5040 + y * (1.0 / 362880)))))
    c = 1.0 + y * (-0.5 + y * (1.0 / 24 + y * (-1.0 / 720 + y * (1.0 / 40320))))
    swap = (quadrant & 1) == 1
    sine = jnp.where(swap, c, s)
    cosine = jnp.where(swap, s, c)
    sine = jnp.where((quadrant & 2) == 2, -sine, sine)
    cosine = jnp.where(((quadrant + 1) & 2) == 2, -cosine, cosine)
    return sine, cosine


def detect_kernel(first, delays, volts, out, spread, rows, weights, *, total):
    dishes, beams = delays.shape
    time = volts.shape[1]
    frequency = first[0] + pl.program_id(0) + total
    sine, cosine = sin_cos(delays[...] * frequency, PHASES)
    scale = jnp.float32(1.0 / math.sqrt(dishes))
    real = (cosine * scale).astype(jnp.bfloat16)
    imag = (-(sine * scale)).astype(jnp.bfloat16)
    width = min(beams, 128)
    for n in range(beams // width):
        cols = slice(n * width, (n + 1) * width)
        weights[n, :dishes, :width] = real[:, cols]
        weights[n, :dishes, width:] = imag[:, cols]
        weights[n, dishes:, :width] = -imag[:, cols]
        weights[n, dishes:, width:] = real[:, cols]
    spread[...] = volts[0].astype(jnp.float32)
    blocks, span, _ = rows.shape
    piece = span // INTEG
    for tb in range(blocks):
        for s in range(INTEG):
            rows[tb, s * piece : (s + 1) * piece, :] = spread[
                pl.ds(tb * span + s, piece, stride=INTEG), :
            ].astype(jnp.bfloat16)
    owners, _, held, _ = out.shape
    for n in range(beams // width):
        parts = []
        for tb in range(blocks):
            beam = jnp.dot(rows[tb], weights[n], preferred_element_type=jnp.float32)
            power = beam[:, :width] * beam[:, :width] + beam[:, width:] * beam[:, width:]
            mean = jnp.sum(power.reshape(INTEG, piece, width), axis=0) * jnp.float32(1.0 / INTEG)
            parts.append(mean)
        series = jnp.concatenate(parts, axis=0).T.astype(jnp.bfloat16)
        share = width // held
        out[n * share : (n + 1) * share, 0, :, :] = series.reshape(share, held, time // INTEG)


def detect(voltages, delays, first, total, owners):
    local, time, doubled = voltages.shape
    dishes, beams = delays.shape
    held = beams // owners
    steps = time // INTEG
    blocks = 8
    width = min(beams, 128)
    return pl.pallas_call(
        lambda *refs: detect_kernel(*refs, total=total),
        grid=(local,),
        in_specs=[
            pl.BlockSpec(memory_space=pltpu.SMEM),
            pl.BlockSpec((dishes, beams), lambda i: (0, 0)),
            pl.BlockSpec((1, time, doubled), lambda i: (i, 0, 0)),
        ],
        out_specs=pl.BlockSpec((owners, 1, held, steps), lambda i: (0, i, 0, 0)),
        out_shape=jax.ShapeDtypeStruct((owners, local, held, steps), jnp.bfloat16),
        scratch_shapes=[
            pltpu.VMEM((time, doubled), jnp.float32),
            pltpu.VMEM((blocks, time // blocks, doubled), jnp.bfloat16),
            pltpu.VMEM((beams // width, doubled, 2 * width), jnp.bfloat16),
        ],
        compiler_params=pltpu.CompilerParams(vmem_limit_bytes=VMEM_LIMIT),
        name="detect",
    )(first.reshape(1), delays, voltages)


def spectra_kernel(series, table, out, wide, rows):
    channels, beams, length = series.shape
    bins = length // 2
    planes, _, lanes = wide.shape
    for q in range(planes):
        piece = series[:, :, q * lanes : (q + 1) * lanes]
        wide[q] = piece.reshape(channels * beams, lanes).astype(jnp.float32)
    for b in range(beams):
        mine = jnp.concatenate(
            [wide[q, pl.ds(b, channels, stride=beams), :] for q in range(planes)], axis=1
        ).astype(jnp.bfloat16)
        rows[b * length : (b + 1) * length, :] = lax.dot_general(
            table[...], mine, (((1,), (1,)), ((), ())), preferred_element_type=jnp.float32
        )

    def gather(k, carry):
        real = rows[pl.ds(k, beams, stride=length), :]
        imag = rows[pl.ds(k + bins, beams, stride=length), :]
        out[k] = jnp.concatenate([real, imag], axis=0).astype(jnp.bfloat16)
        return carry

    lax.fori_loop(0, bins, gather, 0, unroll=8)


def spectra(series, table):
    channels, beams, length = series.shape
    return pl.pallas_call(
        spectra_kernel,
        out_shape=jax.ShapeDtypeStruct((length // 2, 2 * beams, channels), jnp.bfloat16),
        scratch_shapes=[
            pltpu.VMEM((length // 128, channels * beams, 128), jnp.float32),
            pltpu.VMEM((beams * length, channels), jnp.float32),
        ],
        compiler_params=pltpu.CompilerParams(vmem_limit_bytes=VMEM_LIMIT),
        name="spectra",
    )(series, table)


def dedisperse_kernel(shifts, spec, keep, send, cosines, sines, *, start, length, scale):
    step = pl.program_id(0)
    beams = spec.shape[1] // 2
    half = keep.shape[2]

    @pl.when(step == 0)
    def _():
        sine, cosine = sin_cos(shifts[...], length)
        cosines[0] = cosine
        sines[0] = sine

        def extend(j, carry):
            s, c = sines[j - 1], cosines[j - 1]
            cosines[j] = c * cosines[0] - s * sines[0]
            sines[j] = s * cosines[0] + c * sines[0]
            return carry

        lax.fori_loop(1, KBLK, extend, 0)

    base_s, base_c = sin_cos(shifts[...] * (start + step * KBLK), length)
    base_s = base_s * scale
    base_c = base_c * scale

    def one(j, carry):
        c, s = cosines[j], sines[j]
        factor = jnp.concatenate(
            [
                (base_c * c - base_s * s).astype(jnp.bfloat16),
                (base_s * c + base_c * s).astype(jnp.bfloat16),
            ],
            axis=0,
        )
        both = spec[j]
        real = both[:beams]
        imag = both[beams:]
        left = jnp.concatenate(
            [jnp.concatenate([real, -imag], axis=1), jnp.concatenate([imag, real], axis=1)], axis=0
        )
        result = jnp.dot(left, factor, preferred_element_type=jnp.float32).astype(jnp.bfloat16)
        keep[j] = result[:, :half]
        send[j] = result[:, half:]
        return carry

    lax.fori_loop(0, KBLK, one, 0, unroll=2)


def dedisperse(shifts, spec, chunk, chunks, scale):
    bins, rows, channels = spec.shape
    trials = shifts.shape[1]
    count = bins // chunks
    steps = count // KBLK
    shape = jax.ShapeDtypeStruct((count, rows, trials // 2), jnp.bfloat16)
    block = pl.BlockSpec((KBLK, rows, trials // 2), lambda i: (i, 0, 0))
    return pl.pallas_call(
        lambda *refs: dedisperse_kernel(*refs, start=chunk * count, length=2 * bins, scale=scale),
        grid=(steps,),
        in_specs=[
            pl.BlockSpec((channels, trials), lambda i: (0, 0)),
            pl.BlockSpec((KBLK, rows, channels), lambda i: (i + chunk * steps, 0, 0)),
        ],
        out_specs=[block, block],
        out_shape=[shape, shape],
        scratch_shapes=[
            pltpu.VMEM((KBLK, channels, trials), jnp.float32),
            pltpu.VMEM((KBLK, channels, trials), jnp.float32),
        ],
        compiler_params=pltpu.CompilerParams(vmem_limit_bytes=VMEM_LIMIT),
        name=f"dedisperse{chunk}",
    )(shifts, spec)


def dft_table(length):
    bins = length // 2
    row = lax.broadcasted_iota(jnp.int32, (length, length), 0)
    sample = lax.broadcasted_iota(jnp.int32, (length, length), 1)
    sine, cosine = sin_cos(sample * ((row & (bins - 1)) + 1), length)
    return (jnp.where(row < bins, cosine, -sine) * jnp.float32(1.0 / math.sqrt(length))).astype(
        jnp.bfloat16
    )


def fold(values):
    half = values.shape[0] // 2
    return jnp.concatenate([values[:half], values[half:]], axis=-1)


def body(voltages, delays, shifts):
    owners = lax.axis_size("chan")
    groups = lax.axis_size("grp")
    local = voltages.shape[0]
    total = local * owners * groups
    group = lax.axis_index("grp")
    first = (lax.axis_index("chan") * groups + group) * local
    detected = detect(voltages, delays, first, total, owners)
    moved = lax.all_to_all(detected, "chan", split_axis=0, concat_axis=0, tiled=True)
    length = moved.shape[3]
    series = moved.reshape(owners * local, moved.shape[2], length)

    trials = shifts.shape[0]
    block = trials // groups
    mine = lax.dynamic_index_in_dim(
        shifts.reshape(trials, owners, groups, local), group, axis=2, keepdims=False
    ).reshape(groups, block, owners * local)
    ordered = [
        lax.dynamic_index_in_dim(mine, group ^ flip, axis=0, keepdims=False) for flip in (0, 2, 1, 3)
    ]
    shifts_t = jnp.concatenate(ordered, axis=0).T

    spec = spectra(series, dft_table(length))
    scale = 1.0 / math.sqrt(total)
    powers = []
    for chunk in range(CHUNKS):
        keep, send = dedisperse(shifts_t, spec, chunk, CHUNKS, scale)
        got = lax.ppermute(send, "grp", [(g, g ^ 1) for g in range(groups)])
        both = keep.astype(jnp.float32) + got.astype(jnp.float32)
        away = fold(both[:, :, block:]).astype(jnp.bfloat16)
        back = lax.ppermute(away, "grp", [(g, g ^ 2) for g in range(groups)])
        whole = fold(both[:, :, :block]) + back.astype(jnp.float32)
        beams = whole.shape[1] // 2
        power = whole[:, :beams] ** 2 + whole[:, beams:] ** 2
        count = power.shape[0]
        powers.append(power.reshape(count, beams, 2, block).transpose(3, 1, 2, 0).reshape(block, beams, 2 * count))
    return jnp.concatenate(powers, axis=2)


def solution(mesh):
    placed = (P(("chan", "grp"), None, None), P(), P())
    return jax.shard_map(
        body, mesh=mesh, in_specs=placed, out_specs=P("grp", "chan", None), check_vma=False
    )
```

```python
import math

import jax
import jax.numpy as jnp
from jax import lax
from jax.experimental import pallas as pl
from jax.experimental.pallas import tpu as pltpu
from jax.sharding import PartitionSpec as P

INTEG = 8
PHASES = 4096
KBLK = 16
UNITS = (2, 2, 2, 2)
HALVES = 2
VMEM_LIMIT = 56 * 1024 * 1024


def sin_cos(steps, turn):
    quarter = turn // 4
    steps = steps & (turn - 1)
    quadrant = (steps + quarter // 2) >> (quarter.bit_length() - 1)
    x = (steps - quadrant * quarter).astype(jnp.float32) * jnp.float32(2.0 * math.pi / turn)
    y = x * x
    s = x * (1.0 + y * (-1.0 / 6 + y * (1.0 / 120 + y * (-1.0 / 5040 + y * (1.0 / 362880)))))
    c = 1.0 + y * (-0.5 + y * (1.0 / 24 + y * (-1.0 / 720 + y * (1.0 / 40320))))
    swap = (quadrant & 1) == 1
    sine = jnp.where(swap, c, s)
    cosine = jnp.where(swap, s, c)
    sine = jnp.where((quadrant & 2) == 2, -sine, sine)
    cosine = jnp.where(((quadrant + 1) & 2) == 2, -cosine, cosine)
    return sine, cosine


def detect_kernel(first, delays, volts, out, spread, rows, weights, *, total):
    dishes, beams = delays.shape
    time = volts.shape[1]
    frequency = first[0] + pl.program_id(0) + total
    sine, cosine = sin_cos(delays[...] * frequency, PHASES)
    scale = jnp.float32(1.0 / math.sqrt(dishes))
    real = (cosine * scale).astype(jnp.bfloat16)
    imag = (-(sine * scale)).astype(jnp.bfloat16)
    width = min(beams, 128)
    for n in range(beams // width):
        cols = slice(n * width, (n + 1) * width)
        weights[n, :dishes, :width] = real[:, cols]
        weights[n, :dishes, width:] = imag[:, cols]
        weights[n, dishes:, :width] = -imag[:, cols]
        weights[n, dishes:, width:] = real[:, cols]
    spread[...] = volts[0].astype(jnp.float32)
    blocks, span, _ = rows.shape
    piece = span // INTEG
    for tb in range(blocks):
        for s in range(INTEG):
            rows[tb, s * piece : (s + 1) * piece, :] = spread[
                pl.ds(tb * span + s, piece, stride=INTEG), :
            ].astype(jnp.bfloat16)
    owners, _, held, _ = out.shape
    for n in range(beams // width):
        parts = []
        for tb in range(blocks):
            beam = jnp.dot(rows[tb], weights[n], preferred_element_type=jnp.float32)
            power = beam[:, :width] * beam[:, :width] + beam[:, width:] * beam[:, width:]
            mean = jnp.sum(power.reshape(INTEG, piece, width), axis=0) * jnp.float32(1.0 / INTEG)
            parts.append(mean)
        series = jnp.concatenate(parts, axis=0).T.astype(jnp.bfloat16)
        share = width // held
        out[n * share : (n + 1) * share, 0, :, :] = series.reshape(share, held, time // INTEG)


def detect(voltages, delays, first, total, owners, part):
    local, time, doubled = voltages.shape
    time = time // HALVES
    dishes, beams = delays.shape
    held = beams // owners
    steps = time // INTEG
    blocks = 4
    width = min(beams, 128)
    return pl.pallas_call(
        lambda *refs: detect_kernel(*refs, total=total),
        grid=(local,),
        in_specs=[
            pl.BlockSpec(memory_space=pltpu.SMEM),
            pl.BlockSpec((dishes, beams), lambda i: (0, 0)),
            pl.BlockSpec((1, time, doubled), lambda i: (i, part, 0)),
        ],
        out_specs=pl.BlockSpec((owners, 1, held, steps), lambda i: (0, i, 0, 0)),
        out_shape=jax.ShapeDtypeStruct((owners, local, held, steps), jnp.bfloat16),
        scratch_shapes=[
            pltpu.VMEM((time, doubled), jnp.float32),
            pltpu.VMEM((blocks, time // blocks, doubled), jnp.bfloat16),
            pltpu.VMEM((beams // width, doubled, 2 * width), jnp.bfloat16),
        ],
        compiler_params=pltpu.CompilerParams(vmem_limit_bytes=VMEM_LIMIT),
        name=f"detect{part}",
    )(first.reshape(1), delays, voltages)


def transform_rows(series, table, wide):
    channels, beams, _ = series.shape
    planes, _, lanes = wide.shape
    for q in range(planes):
        piece = series[:, :, q * lanes : (q + 1) * lanes]
        wide[q] = piece.reshape(channels * beams, lanes).astype(jnp.float32)
    for b in range(beams):
        mine = jnp.concatenate(
            [wide[q, pl.ds(b, channels, stride=beams), :] for q in range(planes)], axis=1
        ).astype(jnp.bfloat16)
        yield b, lax.dot_general(
            table[...], mine, (((1,), (1,)), ((), ())), preferred_element_type=jnp.float32
        )


def spectra_start_kernel(series, table, out, wide):
    length = table.shape[0]
    for b, product in transform_rows(series, table, wide):
        out[b * length : (b + 1) * length, :] = product


def spectra_end_kernel(series, table, begun, out, wide, rows):
    beams = series.shape[1]
    length = table.shape[0]
    bins = length // 2
    for b, product in transform_rows(series, table, wide):
        span = slice(b * length, (b + 1) * length)
        rows[span, :] = begun[span, :] + product

    def gather(k, carry):
        real = rows[pl.ds(k, beams, stride=length), :]
        imag = rows[pl.ds(k + bins, beams, stride=length), :]
        out[k] = jnp.concatenate([real, imag], axis=0).astype(jnp.bfloat16)
        return carry

    lax.fori_loop(0, bins, gather, 0, unroll=16)


def spectra(series, table, begun=None):
    channels, beams, steps = series.shape
    length = table.shape[0]
    wide = pltpu.VMEM((steps // 128, channels * beams, 128), jnp.float32)
    params = pltpu.CompilerParams(vmem_limit_bytes=VMEM_LIMIT)
    if begun is None:
        return pl.pallas_call(
            spectra_start_kernel,
            out_shape=jax.ShapeDtypeStruct((beams * length, channels), jnp.float32),
            scratch_shapes=[wide],
            compiler_params=params,
            name="spectra_start",
        )(series, table)
    return pl.pallas_call(
        spectra_end_kernel,
        out_shape=jax.ShapeDtypeStruct((length // 2, 2 * beams, channels), jnp.bfloat16),
        scratch_shapes=[wide, pltpu.VMEM((beams * length, channels), jnp.float32)],
        compiler_params=params,
        name="spectra_end",
    )(series, table, begun)


def factors_kernel(shifts, out, cosines, sines, base_c, base_s, *, length, scale):
    step = pl.program_id(0)
    channels = shifts.shape[0]

    @pl.when(step == 0)
    def _():
        sine, cosine = sin_cos(shifts[...], length)
        cosines[0] = cosine
        sines[0] = sine

        def extend(j, carry):
            s, c = sines[j - 1], cosines[j - 1]
            cosines[j] = c * cosines[0] - s * sines[0]
            sines[j] = s * cosines[0] + c * sines[0]
            return carry

        lax.fori_loop(1, KBLK, extend, 0)

    sine, cosine = sin_cos(shifts[...] * (step * KBLK), length)
    base_s[...] = sine * scale
    base_c[...] = cosine * scale
    tile = min(16, channels)

    def one(r, carry):
        at = pl.ds(pl.multiple_of(r * tile, tile), tile)
        below = pl.ds(pl.multiple_of(channels + r * tile, tile), tile)
        bc = base_c[at, :]
        bs = base_s[at, :]
        for j in range(KBLK):
            c = cosines[j, at, :]
            s = sines[j, at, :]
            out[j, at, :] = (bc * c - bs * s).astype(jnp.bfloat16)
            out[j, below, :] = (bs * c + bc * s).astype(jnp.bfloat16)
        return carry

    lax.fori_loop(0, channels // tile, one, 0)


def dedispersion_factors(shifts, length, scale):
    channels, trials = shifts.shape
    bins = length // 2
    return pl.pallas_call(
        lambda *refs: factors_kernel(*refs, length=length, scale=scale),
        grid=(bins // KBLK,),
        in_specs=[pl.BlockSpec((channels, trials), lambda i: (0, 0))],
        out_specs=pl.BlockSpec((KBLK, 2 * channels, trials), lambda i: (i, 0, 0)),
        out_shape=jax.ShapeDtypeStruct((bins, 2 * channels, trials), jnp.bfloat16),
        scratch_shapes=[
            pltpu.VMEM((KBLK, channels, trials), jnp.float32),
            pltpu.VMEM((KBLK, channels, trials), jnp.float32),
            pltpu.VMEM((channels, trials), jnp.float32),
            pltpu.VMEM((channels, trials), jnp.float32),
        ],
        compiler_params=pltpu.CompilerParams(vmem_limit_bytes=VMEM_LIMIT),
        name="factors",
    )(shifts)


def dedisperse_kernel(factors, spec, keep, send):
    beams = spec.shape[1] // 2
    half = keep.shape[2]
    for j in range(KBLK):
        both = spec[j]
        real = both[:beams]
        imag = both[beams:]
        left = jnp.concatenate(
            [jnp.concatenate([real, -imag], axis=1), jnp.concatenate([imag, real], axis=1)], axis=0
        )
        result = jnp.dot(left, factors[j], preferred_element_type=jnp.float32).astype(jnp.bfloat16)
        keep[j] = result[:, :half]
        send[j] = result[:, half:]


def dedisperse(factors, spec, start, units):
    bins, rows, channels = spec.shape
    trials = factors.shape[2]
    middle = bins // (2 * KBLK)
    shape = jax.ShapeDtypeStruct((2 * units * KBLK, rows, trials // 2), jnp.bfloat16)
    block = pl.BlockSpec((KBLK, rows, trials // 2), lambda i: (i, 0, 0))

    def pick(i):
        return (jnp.where(i < units, start + i, middle + start + i - units), 0, 0)

    return pl.pallas_call(
        dedisperse_kernel,
        grid=(2 * units,),
        in_specs=[
            pl.BlockSpec((KBLK, 2 * channels, trials), pick),
            pl.BlockSpec((KBLK, rows, channels), pick),
        ],
        out_specs=[block, block],
        out_shape=[shape, shape],
        compiler_params=pltpu.CompilerParams(vmem_limit_bytes=VMEM_LIMIT),
        name=f"dedisperse{start}",
    )(factors, spec)


def join_kernel(keep, got, own, away):
    count, rows, lanes = own.shape
    both = keep[...].astype(jnp.float32) + got[...].astype(jnp.float32)
    low = both[:count].reshape(count * rows, lanes)
    high = both[count:].reshape(count * rows, lanes)
    near = lax.broadcasted_iota(jnp.int32, low.shape, 1) < lanes // 2
    own[...] = jnp.where(near, low, pltpu.roll(high, lanes // 2, 1)).reshape(own.shape)
    other = jnp.where(near, pltpu.roll(low, lanes // 2, 1), high)
    away[...] = other.astype(jnp.bfloat16).reshape(away.shape)


def join(keep, got, start):
    count, rows, lanes = keep.shape
    return pl.pallas_call(
        join_kernel,
        out_shape=[
            jax.ShapeDtypeStruct((count // 2, rows, lanes), jnp.float32),
            jax.ShapeDtypeStruct((count // 2, rows, lanes), jnp.bfloat16),
        ],
        compiler_params=pltpu.CompilerParams(vmem_limit_bytes=VMEM_LIMIT),
        name=f"join{start}",
    )(keep, got)


def power_kernel(*refs, pieces):
    owns = refs[:pieces]
    backs = refs[pieces : 2 * pieces]
    out, powers, turned = refs[2 * pieces :]
    block, beams, _ = out.shape
    lanes = powers.shape[1]
    at = 0
    for own, back in zip(owns, backs):
        whole = own[...] + back[...].astype(jnp.float32)
        real = whole[:, :beams]
        imag = whole[:, beams:]
        power = real * real + imag * imag
        rows = power.shape[0] * beams
        powers[at : at + rows, :] = power.reshape(rows, lanes)
        at += rows
    count = at // beams
    for b in range(beams):
        flipped = powers[pl.ds(b, count, stride=beams), :].T
        turned[0, b * block : (b + 1) * block, :] = flipped[:block]
        turned[1, b * block : (b + 1) * block, :] = flipped[block:]
    for m in range(block):
        out[m, :, :count] = turned[0, pl.ds(m, beams, stride=block), :]
        out[m, :, count:] = turned[1, pl.ds(m, beams, stride=block), :]


def final_power(owns, backs):
    beams = owns[0].shape[1] // 2
    lanes = owns[0].shape[2]
    count = sum(own.shape[0] for own in owns)
    block = lanes // 2
    return pl.pallas_call(
        lambda *refs: power_kernel(*refs, pieces=len(owns)),
        out_shape=jax.ShapeDtypeStruct((block, beams, 2 * count), jnp.float32),
        scratch_shapes=[
            pltpu.VMEM((count * beams, lanes), jnp.float32),
            pltpu.VMEM((2, beams * block, count), jnp.float32),
        ],
        compiler_params=pltpu.CompilerParams(vmem_limit_bytes=VMEM_LIMIT),
        name="power",
    )(*owns, *backs)


def dft_table(length):
    bins = length // 2
    row = lax.broadcasted_iota(jnp.int32, (length, length), 0)
    sample = lax.broadcasted_iota(jnp.int32, (length, length), 1)
    sine, cosine = sin_cos(sample * ((row & (bins - 1)) + 1), length)
    return (jnp.where(row < bins, cosine, -sine) * jnp.float32(1.0 / math.sqrt(length))).astype(
        jnp.bfloat16
    )


def body(voltages, delays, shifts):
    owners = lax.axis_size("chan")
    groups = lax.axis_size("grp")
    local = voltages.shape[0]
    total = local * owners * groups
    group = lax.axis_index("grp")
    first = (lax.axis_index("chan") * groups + group) * local
    length = voltages.shape[1] // INTEG
    steps = length // HALVES

    series = []
    for part in range(HALVES):
        detected = detect(voltages, delays, first, total, owners, part)
        moved = lax.all_to_all(detected, "chan", split_axis=0, concat_axis=0, tiled=True)
        series.append(moved.reshape(owners * local, moved.shape[2], steps))

    trials = shifts.shape[0]
    block = trials // groups
    mine = lax.dynamic_index_in_dim(
        shifts.reshape(trials, owners, groups, local), group, axis=2, keepdims=False
    ).reshape(groups, block, owners * local)
    ordered = [
        lax.dynamic_index_in_dim(mine, group ^ flip, axis=0, keepdims=False) for flip in (0, 2, 1, 3)
    ]
    shifts_t = jnp.concatenate(ordered, axis=0).T
    factors = dedispersion_factors(shifts_t, length, 1.0 / math.sqrt(total))

    table = dft_table(length)
    begun = spectra(series[0], table[:, :steps])
    spec = spectra(series[1], table[:, steps:], begun)

    owns, backs, sends = [], [], []
    start = 0
    for turn, units in enumerate(UNITS):
        if turn >= 2:
            spec, sends[turn - 2] = lax.optimization_barrier((spec, sends[turn - 2]))
        keep, send = dedisperse(factors, spec, start, units)
        got = lax.ppermute(send, "grp", [(g, g ^ 1) for g in range(groups)])
        own, away = join(keep, got, start)
        owns.append(own)
        sends.append(away)
        start += units
    for away in sends:
        backs.append(lax.ppermute(away, "grp", [(g, g ^ 2) for g in range(groups)]))
    return final_power(owns, backs)


def solution(mesh):
    placed = (P(("chan", "grp"), None, None), P(), P())
    return jax.shard_map(
        body, mesh=mesh, in_specs=placed, out_specs=P("grp", "chan", None), check_vma=False
    )
```

```python
import math

import jax
import jax.numpy as jnp
import numpy as np
from jax import lax
from jax.experimental import pallas as pl
from jax.experimental.pallas import tpu as pltpu
from jax.sharding import PartitionSpec as P

INTEG = 8
PHASES = 4096
BLOCKS = 8
VMEM_LIMIT = 56 * 1024 * 1024
PARAMS = pltpu.CompilerParams(vmem_limit_bytes=VMEM_LIMIT)


def sin_cos(steps, turn):
    quarter = turn // 4
    steps = steps & (turn - 1)
    quadrant = (steps + quarter // 2) >> (quarter.bit_length() - 1)
    x = (steps - quadrant * quarter).astype(jnp.float32) * jnp.float32(2.0 * math.pi / turn)
    y = x * x
    s = x * (1.0 + y * (-1.0 / 6 + y * (1.0 / 120 + y * (-1.0 / 5040 + y * (1.0 / 362880)))))
    c = 1.0 + y * (-0.5 + y * (1.0 / 24 + y * (-1.0 / 720 + y * (1.0 / 40320))))
    swap = (quadrant & 1) == 1
    sine = jnp.where(swap, c, s)
    cosine = jnp.where(swap, s, c)
    sine = jnp.where((quadrant & 2) == 2, -sine, sine)
    cosine = jnp.where(((quadrant + 1) & 2) == 2, -cosine, cosine)
    return sine, cosine


def spectra_kernel(first, delays, table, volts, out, spread, rows, weights, series, mixed, *, total):
    dishes, beams = delays.shape
    channel = pl.program_id(0)
    sine, cosine = sin_cos(delays[...] * (first[0] + channel + total), PHASES)
    scale = jnp.float32(1.0 / math.sqrt(dishes))
    real = (cosine * scale).astype(jnp.bfloat16)
    imag = (-(sine * scale)).astype(jnp.bfloat16)
    width = min(beams, 128)
    tiles = beams // width
    for n in range(tiles):
        cols = slice(n * width, (n + 1) * width)
        weights[n, :dishes, :width] = real[:, cols]
        weights[n, :dishes, width:] = imag[:, cols]
        weights[n, dishes:, :width] = -imag[:, cols]
        weights[n, dishes:, width:] = real[:, cols]
    spread[...] = volts[0].astype(jnp.float32)
    blocks, span, _ = rows.shape
    piece = span // INTEG
    for tb in range(blocks):
        for s in range(INTEG):
            rows[tb, s * piece : (s + 1) * piece, :] = spread[
                pl.ds(tb * span + s, piece, stride=INTEG), :
            ].astype(jnp.bfloat16)
    for n in range(tiles):
        for tb in range(blocks):
            beam = jnp.dot(rows[tb], weights[n], preferred_element_type=jnp.float32)
            power = beam[:, :width] * beam[:, :width] + beam[:, width:] * beam[:, width:]
            mean = jnp.sum(power.reshape(INTEG, piece, width), axis=0) * jnp.float32(1.0 / INTEG)
            series[tb * piece : (tb + 1) * piece, n * width : (n + 1) * width] = mean.astype(
                jnp.bfloat16
            )
    result = jnp.dot(table[...], series[...], preferred_element_type=jnp.float32)
    owners, share, _ = out.shape
    kinds = result.shape[0] // owners
    for kind in range(kinds):
        for n in range(tiles):
            mixed[n, pl.ds(channel * kinds + kind, owners, stride=share), :] = result[
                kind * owners : (kind + 1) * owners, n * width : (n + 1) * width
            ]

    @pl.when(channel == pl.num_programs(0) - 1)
    def _():
        for n in range(tiles):
            out[:, :, n * width : (n + 1) * width] = (
                mixed[n].reshape(owners, share, width).astype(jnp.bfloat16)
            )


def spectra(voltages, delays, table, first, total, devices):
    local, time, doubled = voltages.shape
    dishes, beams = delays.shape
    steps = time // INTEG
    width = min(beams, 128)
    share = local * steps // devices
    return pl.pallas_call(
        lambda *refs: spectra_kernel(*refs, total=total),
        grid=(local,),
        in_specs=[
            pl.BlockSpec(memory_space=pltpu.SMEM),
            pl.BlockSpec((dishes, beams), lambda i: (0, 0)),
            pl.BlockSpec((steps, steps), lambda i: (0, 0)),
            pl.BlockSpec((1, time, doubled), lambda i: (i, 0, 0)),
        ],
        out_specs=pl.BlockSpec((devices, share, beams), lambda i: (0, 0, 0)),
        out_shape=jax.ShapeDtypeStruct((devices, share, beams), jnp.bfloat16),
        scratch_shapes=[
            pltpu.VMEM((time, doubled), jnp.float32),
            pltpu.VMEM((BLOCKS, time // BLOCKS, doubled), jnp.bfloat16),
            pltpu.VMEM((beams // width, doubled, 2 * width), jnp.bfloat16),
            pltpu.VMEM((steps, beams), jnp.bfloat16),
            pltpu.VMEM((beams // width, devices * share, width), jnp.float32),
        ],
        compiler_params=PARAMS,
        name="spectra",
    )(first.reshape(1), delays, table, voltages)


def factors_kernel(device, shifts, out, *, devices, length, scale):
    trials, channels = shifts.shape
    number = pl.program_id(0) * devices + device[0] + 1
    sine, cosine = sin_cos(shifts[...] * number, length)
    sine = (sine * scale).astype(jnp.bfloat16)
    cosine = (cosine * scale).astype(jnp.bfloat16)
    out[0, :trials, :channels] = cosine
    out[0, :trials, channels:] = -sine
    out[0, trials:, :channels] = sine
    out[0, trials:, channels:] = cosine


def dedispersion_factors(shifts, device, devices, length, scale):
    trials, channels = shifts.shape
    held = length // 2 // devices
    return pl.pallas_call(
        lambda *refs: factors_kernel(*refs, devices=devices, length=length, scale=scale),
        grid=(held,),
        in_specs=[
            pl.BlockSpec(memory_space=pltpu.SMEM),
            pl.BlockSpec((trials, channels), lambda i: (0, 0)),
        ],
        out_specs=pl.BlockSpec((1, 2 * trials, 2 * channels), lambda i: (i, 0, 0)),
        out_shape=jax.ShapeDtypeStruct((held, 2 * trials, 2 * channels), jnp.bfloat16),
        compiler_params=PARAMS,
        name="factors",
    )(device.reshape(1), shifts)


def powers_kernel(factors, spec, out, wide, right, powers):
    bins, doubled, _ = factors.shape
    trials = doubled // 2
    devices, share, beams = spec.shape
    tiles, _, width = wide.shape
    channels = right.shape[0] // 2
    kinds = 2 * bins
    for n in range(tiles):
        piece = spec[:, :, n * width : (n + 1) * width]
        wide[n] = piece.reshape(devices * share, width).astype(jnp.float32)
    for h in range(bins):
        for n in range(tiles):
            for part in range(2):
                right[part * channels : (part + 1) * channels, n * width : (n + 1) * width] = wide[
                    n, pl.ds(part * bins + h, channels, stride=kinds), :
                ].astype(jnp.bfloat16)
        result = jnp.dot(factors[h], right[...], preferred_element_type=jnp.float32)
        real = result[:trials]
        imag = result[trials:]
        powers[h] = real * real + imag * imag
    owners, groups, held, lanes = out.shape
    block = trials // groups
    for g in range(groups):
        stack = jnp.concatenate(
            [powers[h, g * block : (g + 1) * block, :] for h in range(bins)], axis=0
        )
        out[:, g] = stack.T.astype(jnp.bfloat16).reshape(owners, held, lanes)


def bin_powers(factors, spec, owners, groups):
    bins, doubled, columns = factors.shape
    devices, share, beams = spec.shape
    width = min(beams, 128)
    trials = doubled // 2
    return pl.pallas_call(
        powers_kernel,
        out_shape=jax.ShapeDtypeStruct(
            (owners, groups, beams // owners, bins * trials // groups), jnp.bfloat16
        ),
        scratch_shapes=[
            pltpu.VMEM((beams // width, devices * share, width), jnp.float32),
            pltpu.VMEM((columns, beams), jnp.bfloat16),
            pltpu.VMEM((bins, trials, beams), jnp.float32),
        ],
        compiler_params=PARAMS,
        name="powers",
    )(factors, spec)


def arrange_kernel(moved, out, wide, turned):
    devices, beams, lanes = moved.shape
    block = out.shape[0]
    tiles, _, width = wide.shape
    each = width // block
    for n in range(tiles):
        piece = moved[:, :, n * width : (n + 1) * width]
        wide[n] = piece.reshape(devices * beams, width).astype(jnp.float32)
    for n in range(tiles):
        for b in range(beams):
            flipped = wide[n, pl.ds(b, devices, stride=beams), :].T
            for e in range(each):
                turned[n * each + e, b * block : (b + 1) * block, :] = flipped[
                    e * block : (e + 1) * block
                ]
    for m in range(block):
        for h in range(tiles * each):
            out[m, :, h * devices : (h + 1) * devices] = turned[
                h, pl.ds(m, beams, stride=block), :
            ]


def arrange(moved, block):
    devices, beams, lanes = moved.shape
    width = 128
    bins = lanes // block
    return pl.pallas_call(
        arrange_kernel,
        out_shape=jax.ShapeDtypeStruct((block, beams, bins * devices), jnp.float32),
        scratch_shapes=[
            pltpu.VMEM((lanes // width, devices * beams, width), jnp.float32),
            pltpu.VMEM((bins, beams * block, devices), jnp.float32),
        ],
        compiler_params=PARAMS,
        name="arrange",
    )(moved)


def dft_table(length):
    sample = np.arange(length)
    angle = (sample * np.arange(1, length // 2 + 1)[:, None]) % length * (2.0 * np.pi / length)
    rows = np.concatenate([np.cos(angle), -np.sin(angle)], axis=0) / math.sqrt(length)
    return jnp.asarray(rows.astype(np.float32)).astype(jnp.bfloat16)


def body(voltages, delays, shifts, table):
    owners = lax.axis_size("chan")
    groups = lax.axis_size("grp")
    devices = owners * groups
    device = lax.axis_index("chan") * groups + lax.axis_index("grp")
    local, time, _ = voltages.shape
    total = local * devices
    length = time // INTEG
    both = ("chan", "grp")

    factors = dedispersion_factors(shifts, device, devices, length, 1.0 / math.sqrt(total))
    sent = spectra(voltages, delays, table, device * local, total, devices)
    spec = lax.all_to_all(sent, both, split_axis=0, concat_axis=0, tiled=True)
    powers = bin_powers(factors, spec, owners, groups)
    powers = powers.reshape((devices,) + powers.shape[2:])
    moved = lax.all_to_all(powers, both, split_axis=0, concat_axis=0, tiled=True)
    return arrange(moved, shifts.shape[0] // groups)


def solution(mesh):
    placed = (P(("chan", "grp"), None, None), P(), P(), P())
    run = jax.shard_map(
        body, mesh=mesh, in_specs=placed, out_specs=P("grp", "chan", None), check_vma=False
    )

    def whole(voltages, delays, shifts):
        return run(voltages, delays, shifts, dft_table(voltages.shape[1] // INTEG))

    return whole
```

```python
import math

import jax
import jax.numpy as jnp
import numpy as np
from jax import lax
from jax.experimental import pallas as pl
from jax.experimental.pallas import tpu as pltpu
from jax.sharding import PartitionSpec as P

INTEG = 8
PHASES = 4096
BLOCKS = 8
VMEM_LIMIT = 56 * 1024 * 1024
PARAMS = pltpu.CompilerParams(vmem_limit_bytes=VMEM_LIMIT)


def sin_cos(steps, turn):
    quarter = turn // 4
    steps = steps & (turn - 1)
    quadrant = (steps + quarter // 2) >> (quarter.bit_length() - 1)
    x = (steps - quadrant * quarter).astype(jnp.float32) * jnp.float32(2.0 * math.pi / turn)
    y = x * x
    s = x * (1.0 + y * (-1.0 / 6 + y * (1.0 / 120 + y * (-1.0 / 5040 + y * (1.0 / 362880)))))
    c = 1.0 + y * (-0.5 + y * (1.0 / 24 + y * (-1.0 / 720 + y * (1.0 / 40320))))
    swap = (quadrant & 1) == 1
    sine = jnp.where(swap, c, s)
    cosine = jnp.where(swap, s, c)
    sine = jnp.where((quadrant & 2) == 2, -sine, sine)
    cosine = jnp.where(((quadrant + 1) & 2) == 2, -cosine, cosine)
    return sine, cosine


def spectra_kernel(first, delays, table, volts, out, spread, rows, weights, series, mixed, *, total):
    dishes, beams = delays.shape
    channel = pl.program_id(0)
    sine, cosine = sin_cos(delays[...] * (first[0] + channel + total), PHASES)
    scale = jnp.float32(1.0 / math.sqrt(dishes))
    real = (cosine * scale).astype(jnp.bfloat16)
    imag = (-(sine * scale)).astype(jnp.bfloat16)
    width = min(beams, 128)
    tiles = beams // width
    for n in range(tiles):
        cols = slice(n * width, (n + 1) * width)
        weights[n, :dishes, :width] = real[:, cols]
        weights[n, :dishes, width:] = imag[:, cols]
        weights[n, dishes:, :width] = -imag[:, cols]
        weights[n, dishes:, width:] = real[:, cols]
    spread[...] = volts[0].astype(jnp.float32)
    blocks, span, _ = rows.shape
    piece = span // INTEG
    for tb in range(blocks):
        for s in range(INTEG):
            rows[tb, s * piece : (s + 1) * piece, :] = spread[
                pl.ds(tb * span + s, piece, stride=INTEG), :
            ].astype(jnp.bfloat16)
    for n in range(tiles):
        for tb in range(blocks):
            beam = jnp.dot(rows[tb], weights[n], preferred_element_type=jnp.float32)
            power = beam[:, :width] * beam[:, :width] + beam[:, width:] * beam[:, width:]
            mean = jnp.sum(power.reshape(INTEG, piece, width), axis=0) * jnp.float32(1.0 / INTEG)
            series[tb * piece : (tb + 1) * piece, n * width : (n + 1) * width] = mean.astype(
                jnp.bfloat16
            )
    result = jnp.dot(table[...], series[...], preferred_element_type=jnp.float32)
    owners, share, _ = out.shape
    kinds = result.shape[0] // owners
    local = share // kinds
    for kind in range(kinds):
        part, h = divmod(kind, kinds // 2)
        row = (2 * h + part) * local + channel
        for n in range(tiles):
            mixed[n, pl.ds(row, owners, stride=share), :] = result[
                kind * owners : (kind + 1) * owners, n * width : (n + 1) * width
            ]

    @pl.when(channel == pl.num_programs(0) - 1)
    def _():
        for n in range(tiles):
            out[:, :, n * width : (n + 1) * width] = (
                mixed[n].reshape(owners, share, width).astype(jnp.bfloat16)
            )


def spectra(voltages, delays, table, first, total, devices):
    local, time, doubled = voltages.shape
    dishes, beams = delays.shape
    steps = time // INTEG
    width = min(beams, 128)
    share = local * steps // devices
    return pl.pallas_call(
        lambda *refs: spectra_kernel(*refs, total=total),
        grid=(local,),
        in_specs=[
            pl.BlockSpec(memory_space=pltpu.SMEM),
            pl.BlockSpec((dishes, beams), lambda i: (0, 0)),
            pl.BlockSpec((steps, steps), lambda i: (0, 0)),
            pl.BlockSpec((1, time, doubled), lambda i: (i, 0, 0)),
        ],
        out_specs=pl.BlockSpec((devices, share, beams), lambda i: (0, 0, 0)),
        out_shape=jax.ShapeDtypeStruct((devices, share, beams), jnp.bfloat16),
        scratch_shapes=[
            pltpu.VMEM((time, doubled), jnp.float32),
            pltpu.VMEM((BLOCKS, time // BLOCKS, doubled), jnp.bfloat16),
            pltpu.VMEM((beams // width, doubled, 2 * width), jnp.bfloat16),
            pltpu.VMEM((steps, beams), jnp.bfloat16),
            pltpu.VMEM((beams // width, devices * share, width), jnp.float32),
        ],
        compiler_params=PARAMS,
        name="spectra",
    )(first.reshape(1), delays, table, voltages)


def factors_kernel(device, shifts, out, *, devices, length, scale, local):
    trials, columns = shifts.shape
    number = pl.program_id(0) * devices + device[0] + 1
    sine, cosine = sin_cos(shifts[...] * number, length)
    sine = sine * scale
    cosine = cosine * scale
    column = lax.broadcasted_iota(jnp.int32, (trials, columns), 1)
    real = (column & local) == 0
    out[0, :trials] = jnp.where(real, cosine, -sine).astype(jnp.bfloat16)
    out[0, trials:] = jnp.where(real, sine, cosine).astype(jnp.bfloat16)


def dedispersion_factors(shifts, device, devices, length, scale):
    trials, channels = shifts.shape
    held = length // 2 // devices
    local = channels // devices
    columns = 2 * channels
    doubled = jnp.broadcast_to(
        shifts.reshape(trials, devices, 1, local), (trials, devices, 2, local)
    ).reshape(trials, columns)
    return pl.pallas_call(
        lambda *refs: factors_kernel(
            *refs, devices=devices, length=length, scale=scale, local=local
        ),
        grid=(held,),
        in_specs=[
            pl.BlockSpec(memory_space=pltpu.SMEM),
            pl.BlockSpec((trials, columns), lambda i: (0, 0)),
        ],
        out_specs=pl.BlockSpec((1, 2 * trials, columns), lambda i: (i, 0, 0)),
        out_shape=jax.ShapeDtypeStruct((held, 2 * trials, columns), jnp.bfloat16),
        compiler_params=PARAMS,
        name="factors",
    )(device.reshape(1), doubled)


def powers_kernel(stored, spec, out, right, powers, factors, arrived):
    bins, doubled, columns = factors.shape
    trials = doubled // 2
    devices, share, beams = spec.shape
    width = min(beams, 128)
    each = share // bins
    fetches = [
        pltpu.make_async_copy(stored.at[h], factors.at[h], arrived.at[h]) for h in range(bins)
    ]
    for fetch in fetches:
        fetch.start()
    for n in range(beams // width):
        cols = slice(n * width, (n + 1) * width)
        piece = spec[:, :, cols].astype(jnp.float32)
        for h in range(bins):
            right[h, :, cols] = (
                piece[:, h * each : (h + 1) * each].reshape(columns, width).astype(jnp.bfloat16)
            )
    for h in range(bins):
        fetches[h].wait()
        result = jnp.dot(factors[h], right[h], preferred_element_type=jnp.float32)
        real = result[:trials]
        imag = result[trials:]
        powers[h] = real * real + imag * imag
    owners, groups, held, lanes = out.shape
    block = trials // groups
    for g in range(groups):
        stack = jnp.concatenate(
            [powers[h, g * block : (g + 1) * block, :] for h in range(bins)], axis=0
        )
        out[:, g] = stack.T.astype(jnp.bfloat16).reshape(owners, held, lanes)


def bin_powers(factors, spec, owners, groups):
    bins, doubled, columns = factors.shape
    beams = spec.shape[2]
    trials = doubled // 2
    return pl.pallas_call(
        powers_kernel,
        in_specs=[pl.BlockSpec(memory_space=pl.ANY), pl.BlockSpec(memory_space=pltpu.VMEM)],
        out_shape=pltpu.VMEM(
            (owners, groups, beams // owners, bins * trials // groups), jnp.bfloat16
        ),
        scratch_shapes=[
            pltpu.VMEM((bins, columns, beams), jnp.bfloat16),
            pltpu.VMEM((bins, trials, beams), jnp.float32),
            pltpu.VMEM(factors.shape, jnp.bfloat16),
            pltpu.SemaphoreType.DMA((bins,)),
        ],
        compiler_params=PARAMS,
        name="powers",
    )(factors, spec)


def arrange_kernel(moved, out, wide, turned):
    devices, beams, lanes = moved.shape
    block = out.shape[0]
    tiles, _, width = wide.shape
    each = width // block
    for n in range(tiles):
        piece = moved[:, :, n * width : (n + 1) * width]
        wide[n] = piece.reshape(devices * beams, width).astype(jnp.float32)
    for n in range(tiles):
        for b in range(beams):
            flipped = wide[n, pl.ds(b, devices, stride=beams), :].T
            for e in range(each):
                turned[n * each + e, b * block : (b + 1) * block, :] = flipped[
                    e * block : (e + 1) * block
                ]
    for m in range(block):
        for h in range(tiles * each):
            out[m, :, h * devices : (h + 1) * devices] = turned[
                h, pl.ds(m, beams, stride=block), :
            ]


def arrange(moved, block):
    devices, beams, lanes = moved.shape
    width = 128
    bins = lanes // block
    return pl.pallas_call(
        arrange_kernel,
        out_shape=jax.ShapeDtypeStruct((block, beams, bins * devices), jnp.float32),
        scratch_shapes=[
            pltpu.VMEM((lanes // width, devices * beams, width), jnp.float32),
            pltpu.VMEM((bins, beams * block, devices), jnp.float32),
        ],
        compiler_params=PARAMS,
        name="arrange",
    )(moved)


def dft_table(length):
    sample = np.arange(length)
    angle = (sample * np.arange(1, length // 2 + 1)[:, None]) % length * (2.0 * np.pi / length)
    rows = np.concatenate([np.cos(angle), -np.sin(angle)], axis=0) / math.sqrt(length)
    return jnp.asarray(rows.astype(np.float32)).astype(jnp.bfloat16)


def body(voltages, delays, shifts, table):
    owners = lax.axis_size("chan")
    groups = lax.axis_size("grp")
    devices = owners * groups
    device = lax.axis_index("chan") * groups + lax.axis_index("grp")
    local, time, _ = voltages.shape
    total = local * devices
    length = time // INTEG
    both = ("chan", "grp")

    factors = dedispersion_factors(shifts, device, devices, length, 1.0 / math.sqrt(total))
    sent = spectra(voltages, delays, table, device * local, total, devices)
    spec = lax.all_to_all(sent, both, split_axis=0, concat_axis=0, tiled=True)
    spec = pltpu.with_memory_space_constraint(spec, pltpu.VMEM)
    powers = bin_powers(factors, spec, owners, groups)
    powers = powers.reshape((devices,) + powers.shape[2:])
    moved = lax.all_to_all(powers, both, split_axis=0, concat_axis=0, tiled=True)
    moved = pltpu.with_memory_space_constraint(moved, pltpu.VMEM)
    return arrange(moved, shifts.shape[0] // groups)


def solution(mesh):
    placed = (P(("chan", "grp"), None, None), P(), P(), P())
    run = jax.shard_map(
        body, mesh=mesh, in_specs=placed, out_specs=P("grp", "chan", None), check_vma=False
    )

    def whole(voltages, delays, shifts):
        return run(voltages, delays, shifts, dft_table(voltages.shape[1] // INTEG))

    return whole
```

```python
import math

import jax
import jax.numpy as jnp
import numpy as np
from jax import lax
from jax.experimental import pallas as pl
from jax.experimental.pallas import tpu as pltpu
from jax.sharding import PartitionSpec as P

INTEG = 8
PHASES = 4096
BLOCKS = 8
PIECES = 8
VMEM_LIMIT = 56 * 1024 * 1024
PARAMS = pltpu.CompilerParams(vmem_limit_bytes=VMEM_LIMIT)


def sin_cos(steps, turn):
    quarter = turn // 4
    steps = steps & (turn - 1)
    quadrant = (steps + quarter // 2) >> (quarter.bit_length() - 1)
    x = (steps - quadrant * quarter).astype(jnp.float32) * jnp.float32(2.0 * math.pi / turn)
    y = x * x
    s = x * (1.0 + y * (-1.0 / 6 + y * (1.0 / 120 + y * (-1.0 / 5040 + y * (1.0 / 362880)))))
    c = 1.0 + y * (-0.5 + y * (1.0 / 24 + y * (-1.0 / 720 + y * (1.0 / 40320))))
    swap = (quadrant & 1) == 1
    sine = jnp.where(swap, c, s)
    cosine = jnp.where(swap, s, c)
    sine = jnp.where((quadrant & 2) == 2, -sine, sine)
    cosine = jnp.where(((quadrant + 1) & 2) == 2, -cosine, cosine)
    return sine, cosine


def spectra_kernel(
    first, delays, stored, volts, out, spread, rows, weights, series, mixed, staged, table, arrived,
    written, *, total
):
    dishes, beams = delays.shape
    channel = pl.program_id(0)
    fetch = pltpu.make_async_copy(stored, table, arrived)

    @pl.when(channel == 0)
    def _():
        fetch.start()

    sine, cosine = sin_cos(delays[...] * (first[0] + channel + total), PHASES)
    scale = jnp.float32(1.0 / math.sqrt(dishes))
    real = (cosine * scale).astype(jnp.bfloat16)
    imag = (-(sine * scale)).astype(jnp.bfloat16)
    width = min(beams, 128)
    tiles = beams // width
    for n in range(tiles):
        cols = slice(n * width, (n + 1) * width)
        weights[n, :dishes, :width] = real[:, cols]
        weights[n, :dishes, width:] = imag[:, cols]
        weights[n, dishes:, :width] = -imag[:, cols]
        weights[n, dishes:, width:] = real[:, cols]
    spread[...] = volts[0].astype(jnp.float32)
    blocks, span, _ = rows.shape
    piece = span // INTEG
    for tb in range(blocks):
        for s in range(INTEG):
            rows[tb, s * piece : (s + 1) * piece, :] = spread[
                pl.ds(tb * span + s, piece, stride=INTEG), :
            ].astype(jnp.bfloat16)
    for n in range(tiles):
        for tb in range(blocks):
            beam = jnp.dot(rows[tb], weights[n], preferred_element_type=jnp.float32)
            power = beam[:, :width] * beam[:, :width] + beam[:, width:] * beam[:, width:]
            mean = jnp.sum(power.reshape(INTEG, piece, width), axis=0) * jnp.float32(1.0 / INTEG)
            series[tb * piece : (tb + 1) * piece, n * width : (n + 1) * width] = mean.astype(
                jnp.bfloat16
            )

    @pl.when(channel == 0)
    def _():
        fetch.wait()

    result = jnp.dot(table[...], series[...], preferred_element_type=jnp.float32)
    owners, share, _ = out.shape
    kinds = result.shape[0] // owners
    local = share // kinds
    for kind in range(kinds):
        part, h = divmod(kind, kinds // 2)
        row = (2 * h + part) * local + channel
        for n in range(tiles):
            mixed[n, pl.ds(row, owners, stride=share), :] = result[
                kind * owners : (kind + 1) * owners, n * width : (n + 1) * width
            ]

    @pl.when(channel == pl.num_programs(0) - 1)
    def _():
        count = owners // PIECES
        copies = []
        for q in range(PIECES):
            span = slice(q * count, (q + 1) * count)
            for n in range(tiles):
                piece = mixed[n, q * count * share : (q + 1) * count * share, :]
                staged[span, :, n * width : (n + 1) * width] = piece.reshape(
                    count, share, width
                ).astype(jnp.bfloat16)
            copies.append(pltpu.make_async_copy(staged.at[span], out.at[span], written.at[q]))
            copies[-1].start()
        for copy in copies:
            copy.wait()


def spectra(voltages, delays, table, first, total, devices):
    local, time, doubled = voltages.shape
    dishes, beams = delays.shape
    steps = time // INTEG
    width = min(beams, 128)
    share = local * steps // devices
    return pl.pallas_call(
        lambda *refs: spectra_kernel(*refs, total=total),
        grid=(local,),
        in_specs=[
            pl.BlockSpec(memory_space=pltpu.SMEM),
            pl.BlockSpec((dishes, beams), lambda i: (0, 0)),
            pl.BlockSpec(memory_space=pl.ANY),
            pl.BlockSpec((1, time, doubled), lambda i: (i, 0, 0)),
        ],
        out_specs=pl.BlockSpec(memory_space=pl.ANY),
        out_shape=jax.ShapeDtypeStruct((devices, share, beams), jnp.bfloat16),
        scratch_shapes=[
            pltpu.VMEM((time, doubled), jnp.float32),
            pltpu.VMEM((BLOCKS, time // BLOCKS, doubled), jnp.bfloat16),
            pltpu.VMEM((beams // width, doubled, 2 * width), jnp.bfloat16),
            pltpu.VMEM((steps, beams), jnp.bfloat16),
            pltpu.VMEM((beams // width, devices * share, width), jnp.float32),
            pltpu.VMEM((devices, share, beams), jnp.bfloat16),
            pltpu.VMEM((steps, steps), jnp.bfloat16),
            pltpu.SemaphoreType.DMA,
            pltpu.SemaphoreType.DMA((PIECES,)),
        ],
        compiler_params=PARAMS,
        name="spectra",
    )(first.reshape(1), delays, table, voltages)


def factors_kernel(device, shifts, out, *, devices, length, scale, local):
    trials, columns = shifts.shape
    number = pl.program_id(0) * devices + device[0] + 1
    sine, cosine = sin_cos(shifts[...] * number, length)
    sine = sine * scale
    cosine = cosine * scale
    column = lax.broadcasted_iota(jnp.int32, (trials, columns), 1)
    real = (column & local) == 0
    out[0, :trials] = jnp.where(real, cosine, -sine).astype(jnp.bfloat16)
    out[0, trials:] = jnp.where(real, sine, cosine).astype(jnp.bfloat16)


def dedispersion_factors(shifts, device, devices, length, scale):
    trials, channels = shifts.shape
    held = length // 2 // devices
    local = channels // devices
    columns = 2 * channels
    doubled = jnp.broadcast_to(
        shifts.reshape(trials, devices, 1, local), (trials, devices, 2, local)
    ).reshape(trials, columns)
    return pl.pallas_call(
        lambda *refs: factors_kernel(
            *refs, devices=devices, length=length, scale=scale, local=local
        ),
        grid=(held,),
        in_specs=[
            pl.BlockSpec(memory_space=pltpu.SMEM),
            pl.BlockSpec((trials, columns), lambda i: (0, 0)),
        ],
        out_specs=pl.BlockSpec((1, 2 * trials, columns), lambda i: (i, 0, 0)),
        out_shape=jax.ShapeDtypeStruct((held, 2 * trials, columns), jnp.bfloat16),
        compiler_params=PARAMS,
        name="factors",
    )(device.reshape(1), doubled)


def powers_kernel(stored, spec, out, right, powers, factors, arrived):
    bins, doubled, columns = factors.shape
    trials = doubled // 2
    devices, share, beams = spec.shape
    width = min(beams, 128)
    each = share // bins
    fetches = [
        pltpu.make_async_copy(stored.at[h], factors.at[h], arrived.at[h]) for h in range(bins)
    ]
    for fetch in fetches:
        fetch.start()
    for n in range(beams // width):
        cols = slice(n * width, (n + 1) * width)
        piece = spec[:, :, cols].astype(jnp.float32)
        for h in range(bins):
            right[h, :, cols] = (
                piece[:, h * each : (h + 1) * each].reshape(columns, width).astype(jnp.bfloat16)
            )
    for h in range(bins):
        fetches[h].wait()
        result = jnp.dot(factors[h], right[h], preferred_element_type=jnp.float32)
        real = result[:trials]
        imag = result[trials:]
        powers[h] = real * real + imag * imag
    owners, groups, held, lanes = out.shape
    block = trials // groups
    for g in range(groups):
        stack = jnp.concatenate(
            [powers[h, g * block : (g + 1) * block, :] for h in range(bins)], axis=0
        )
        out[:, g] = stack.T.astype(jnp.bfloat16).reshape(owners, held, lanes)


def bin_powers(factors, spec, owners, groups):
    bins, doubled, columns = factors.shape
    beams = spec.shape[2]
    trials = doubled // 2
    return pl.pallas_call(
        powers_kernel,
        in_specs=[pl.BlockSpec(memory_space=pl.ANY), pl.BlockSpec(memory_space=pltpu.VMEM)],
        out_shape=pltpu.VMEM(
            (owners, groups, beams // owners, bins * trials // groups), jnp.bfloat16
        ),
        scratch_shapes=[
            pltpu.VMEM((bins, columns, beams), jnp.bfloat16),
            pltpu.VMEM((bins, trials, beams), jnp.float32),
            pltpu.VMEM(factors.shape, jnp.bfloat16),
            pltpu.SemaphoreType.DMA((bins,)),
        ],
        compiler_params=PARAMS,
        name="powers",
    )(factors, spec)


def arrange_kernel(moved, out, wide, turned):
    devices, beams, lanes = moved.shape
    block = out.shape[0]
    tiles, _, width = wide.shape
    each = width // block
    for n in range(tiles):
        piece = moved[:, :, n * width : (n + 1) * width]
        wide[n] = piece.reshape(devices * beams, width).astype(jnp.float32)
    for n in range(tiles):
        for b in range(beams):
            flipped = wide[n, pl.ds(b, devices, stride=beams), :].T
            for e in range(each):
                turned[n * each + e, b * block : (b + 1) * block, :] = flipped[
                    e * block : (e + 1) * block
                ]
    for m in range(block):
        for h in range(tiles * each):
            out[m, :, h * devices : (h + 1) * devices] = turned[
                h, pl.ds(m, beams, stride=block), :
            ]


def arrange(moved, block):
    devices, beams, lanes = moved.shape
    width = 128
    bins = lanes // block
    return pl.pallas_call(
        arrange_kernel,
        out_shape=jax.ShapeDtypeStruct((block, beams, bins * devices), jnp.float32),
        scratch_shapes=[
            pltpu.VMEM((lanes // width, devices * beams, width), jnp.float32),
            pltpu.VMEM((bins, beams * block, devices), jnp.float32),
        ],
        compiler_params=PARAMS,
        name="arrange",
    )(moved)


def dft_table(length):
    sample = np.arange(length)
    angle = (sample * np.arange(1, length // 2 + 1)[:, None]) % length * (2.0 * np.pi / length)
    rows = np.concatenate([np.cos(angle), -np.sin(angle)], axis=0) / math.sqrt(length)
    return jnp.asarray(rows.astype(np.float32)).astype(jnp.bfloat16)


def body(voltages, delays, shifts, table):
    owners = lax.axis_size("chan")
    groups = lax.axis_size("grp")
    devices = owners * groups
    device = lax.axis_index("chan") * groups + lax.axis_index("grp")
    local, time, _ = voltages.shape
    total = local * devices
    length = time // INTEG
    both = ("chan", "grp")

    factors = dedispersion_factors(shifts, device, devices, length, 1.0 / math.sqrt(total))
    sent = spectra(voltages, delays, table, device * local, total, devices)
    spec = lax.all_to_all(sent, both, split_axis=0, concat_axis=0, tiled=True)
    spec = pltpu.with_memory_space_constraint(spec, pltpu.VMEM)
    powers = bin_powers(factors, spec, owners, groups)
    powers = powers.reshape((devices,) + powers.shape[2:])
    moved = lax.all_to_all(powers, both, split_axis=0, concat_axis=0, tiled=True)
    moved = pltpu.with_memory_space_constraint(moved, pltpu.VMEM)
    return arrange(moved, shifts.shape[0] // groups)


def solution(mesh):
    placed = (P(("chan", "grp"), None, None), P(), P(), P())
    run = jax.shard_map(
        body, mesh=mesh, in_specs=placed, out_specs=P("grp", "chan", None), check_vma=False
    )

    def whole(voltages, delays, shifts):
        return run(voltages, delays, shifts, dft_table(voltages.shape[1] // INTEG))

    return whole
```
